32 devices in a mesh: groups: 2 (over x), wide: 8 (over z, y), narrow: 2 (over core).
Axes of the slice: x: 2, y: 2, z: 4, core: 2. Of those that a mesh axis runs over, the one named last changes fastest.
Arguments:
- tokens: bfloat16 [2048, 2048], P(('groups', 'wide', 'narrow')), parts along dimension 0, may hold values from -6 to 6
- gate_wts: bfloat16 [2048, 8], P(('groups', 'wide', 'narrow')), parts along dimension 0, may hold values from 0.099609375 to 1
- expert_ids: int32 [2048, 8], P(('groups', 'wide', 'narrow')), parts along dimension 0, may hold values from 0 to 23, as said below
- replica: int32 [2048, 8], P(('groups', 'wide', 'narrow')), parts along dimension 0, may hold values from 0 to 1, as said below
- w_gate: bfloat16 [32, 2048, 384], P(('wide', 'narrow')), may hold values from -0.125 to 0.125
- w_up: bfloat16 [32, 2048, 384], P(('wide', 'narrow')), may hold values from -0.125 to 0.125
- w_down: bfloat16 [32, 384, 2048], P(('wide', 'narrow')), may hold values from -0.3125 to 0.3125
- queries: bfloat16 [64, 32, 128], P(('groups', 'wide', 'narrow')), parts along dimension 0, may hold values from -80 to 80
- k_cache: bfloat16 [64, 640, 4, 128], P(('groups', 'wide', 'narrow')), parts along dimension 0, may hold values from -4 to 4
- value_cache: bfloat16 [64, 640, 4, 128], P(('groups', 'wide', 'narrow')), parts along dimension 0, may hold values from -5 to 5
- lengths: int32 [64], P(('groups', 'wide', 'narrow')), parts along dimension 0, may hold values from 80 to 640, as said below
Outputs:
- routed_out: bfloat16 [2048, 2048], P(('groups', 'wide', 'narrow')), parts along dimension 0
- attn_out: bfloat16 [64, 4096], P(('groups', 'wide', 'narrow')), parts along dimension 0
The draws below stay inside these ranges and needn't reach their ends.
There are 2 independent parts, one for each index of `groups`. The reference program is written for one: setup_inputs(seed, part) draws one part's arguments, and reference() takes and returns one part's arrays. A program takes and returns all parts, laid end to end along the dimension named above; an argument that names none is the same for every part. Nothing has to cross between parts.
Inputs may be any that keep to these rules, and one draw needn't show every extreme that they name: `expert_ids`: each row names 8 different experts. Counted over the rows of one device (aligned blocks of 64 rows), the rows whose slots lie on one device number at most 64; one device, the same for every block of a draw, gets exactly 64 rows from every block. `replica`: 1 only where the named expert is below 8. `lengths`: one request of each draw has exactly 640 live positions.
All inputs are finite; a program needn't handle non-finite values.
Results may differ from the reference program's by a relative error of at most 0.008.
Values may be sent and summed in bfloat16 or wider, within the bound.
No kernel may reach another device: no remote copies, remote signals or barrier semaphores. Data moves between devices by JAX's collectives and lax.ppermute only.
A program may use at most 128 MiB of HBM per device.

```python
import math
import jax
import jax.numpy as jnp
from jax import lax

D = 2048
HE = 384
TOPK = 8
SLOT_DEV = 2
QUERY_HEADS = 32
KEY_VALUE_HEADS = 4
HEAD_SIZE = 128
CACHE_POSITIONS = 640
ROWS = 64
DEVS_PART = 16
EXPERTS = 24
REPLICAS = 8
SLOTS = 32
CAP = 64
TOKENS = 1024
REQUEST_COUNT = 32


def route_slots(key):
    key = jax.random.fold_in(key, 11)
    first, second = jax.random.split(key, 2)
    quarter = DEVS_PART // 4
    upper = 3 * DEVS_PART // 4
    pairs_total = ROWS * TOPK
    remaining = pairs_total - 2 * CAP
    even_share = remaining // (DEVS_PART - 1)
    spare_cut = remaining % (DEVS_PART - 1)
    hottest = quarter + jax.random.randint(first, (), 0, DEVS_PART // 2)
    devices = jnp.arange(DEVS_PART, dtype=jnp.int32)
    unit_of = jnp.where(devices >= upper, devices - upper, devices).astype(jnp.int32)
    is_upper = (devices >= upper).astype(jnp.int32)
    position = jnp.arange(DEVS_PART, dtype=jnp.int32)
    counts = jnp.where(position == 0, 2 * CAP, even_share + (position - 1 < spare_cut).astype(jnp.int32)).astype(jnp.int32)
    bounds = jnp.cumsum(counts)
    pairs = jnp.arange(pairs_total, dtype=jnp.int32)
    place = jnp.sum((bounds[None, :] <= pairs[:, None]).astype(jnp.int32), axis=1).astype(jnp.int32)
    within = pairs % (2 * ROWS)
    row_of = within // 2
    col_of = 2 * (pairs // (2 * ROWS)) + pairs % 2
    bit_of = pairs % 2

    def block(block_key):
        key_first_split, key_second_split = jax.random.split(block_key, 2)
        ranking = jax.random.permutation(key_first_split, upper).astype(jnp.int32)[unit_of]
        score = jnp.where(devices == hottest, -1, 2 * ranking + is_upper).astype(jnp.int32)
        sequence = jnp.argsort(score, stable=True).astype(jnp.int32)
        dev_of = sequence[place]
        slots_blk = jnp.zeros((ROWS, TOPK), jnp.int32).at[row_of, col_of].set(SLOT_DEV * dev_of + bit_of)
        shuffle = jax.random.permutation(key_second_split, ROWS)
        return slots_blk[shuffle]
    keys = jax.random.split(second, DEVS_PART)
    return lax.map(block, keys).reshape(TOKENS, TOPK).astype(jnp.int32)


def draw_expert_ids(key, part):
    slots_all = route_slots(key)
    return jnp.where(slots_all >= EXPERTS, slots_all - EXPERTS, slots_all).astype(jnp.int32)


def draw_replica(key, part):
    slots_all = route_slots(key)
    return (slots_all >= EXPERTS).astype(jnp.int32)


def draw_lengths(key, part):
    key = jax.random.fold_in(key, 5)
    key_first_split, key_second_split = jax.random.split(key, 2)
    value_rows = jax.random.randint(key_first_split, (REQUEST_COUNT,), CACHE_POSITIONS // 8, CACHE_POSITIONS + 1)
    where_full = jax.random.randint(key_second_split, (), 0, REQUEST_COUNT)
    return value_rows.at[where_full].set(CACHE_POSITIONS).astype(jnp.int32)


def draw_k_cache(key, part):
    inner_product = jax.random.fold_in(key, 1)
    value_rows = jnp.clip(jax.random.normal(inner_product, (REQUEST_COUNT, CACHE_POSITIONS, KEY_VALUE_HEADS, HEAD_SIZE), jnp.float32), -4.0, 4.0)
    return value_rows.astype(jnp.bfloat16)


def draw_queries(key, part):
    inner_product = jax.random.fold_in(key, 2)
    value_rows = jnp.clip(jax.random.normal(inner_product, (REQUEST_COUNT, QUERY_HEADS, HEAD_SIZE), jnp.float32), -4.0, 4.0)
    return value_rows.astype(jnp.bfloat16)


def level_of(own_key, extent, pieces, smallest, top_value):
    loudness, own = 1.0, jax.random.fold_in(own_key, 6)
    for dim, parts in pieces:
        steps = jnp.exp(jax.random.uniform(jax.random.fold_in(own, dim), (parts,), jnp.float32, smallest / len(pieces), top_value / len(pieces)))
        loudness = loudness * jnp.repeat(steps, extent[dim] // parts).reshape([-1 if axis == dim else 1 for axis in range(len(extent))])
    return loudness


def centred(own_key, extent, width, reach, cuts=(), kind=jnp.bfloat16):
    gain = level_of(own_key, extent, cuts, -0.22, 0.18) if cuts else 1.0
    values = jax.random.normal(own_key, extent, jnp.float32) * width * gain
    return jnp.minimum(jnp.maximum(values, -reach), reach).astype(kind)


def setup_inputs(seed: int = 0, part: int = 0) -> dict:
    arg_keys = jax.random.split(jax.random.key(seed), 12)
    part_splits = jax.random.split(jax.random.fold_in(arg_keys[11], part), 12)
    return {
        "tokens": centred(part_splits[0], (TOKENS, D), 1.0, 6.0, ((0, 16),)),
        "gate_wts": jnp.clip(jnp.exp(math.log(1.0) - 2.306499 * jax.random.uniform(part_splits[1], (TOKENS, TOPK), jnp.float32) ** level_of(part_splits[1], (TOKENS, TOPK), ((0, 16),), -0.2, 0.2)), 0.099609375, 1.0).astype(jnp.bfloat16),
        "expert_ids": draw_expert_ids(jax.random.fold_in(jax.random.fold_in(arg_keys[11], part), 71), part),
        "replica": draw_replica(jax.random.fold_in(jax.random.fold_in(arg_keys[11], part), 71), part),
        "w_gate": centred(arg_keys[4], (SLOTS, D, HE), D ** -0.5, 0.125, ((0, 16),)),
        "w_up": centred(arg_keys[5], (SLOTS, D, HE), D ** -0.5, 0.125, ((0, 16),)),
        "w_down": centred(arg_keys[6], (SLOTS, HE, D), HE ** -0.5, 0.3125, ((0, 16),)),
        "queries": draw_queries(jax.random.fold_in(jax.random.fold_in(arg_keys[11], part), 71), part),
        "k_cache": draw_k_cache(jax.random.fold_in(jax.random.fold_in(arg_keys[11], part), 71), part),
        "value_cache": centred(part_splits[9], (REQUEST_COUNT, CACHE_POSITIONS, KEY_VALUE_HEADS, HEAD_SIZE), 1.0, 5.0, ((0, 16),)),
        "lengths": draw_lengths(jax.random.fold_in(jax.random.fold_in(arg_keys[11], part), 71), part),
    }


def attend(queries, k_cache, value_cache, lengths):
    reqs, heads, head_dim = queries.shape
    kv_heads = k_cache.shape[2]
    group = heads // kv_heads
    grouped = queries.reshape(reqs, kv_heads, group, head_dim).astype(jnp.float32)
    scores = jnp.einsum("rkgd,rlkd->rkgl", grouped, k_cache.astype(jnp.float32)) * (head_dim ** -0.5)
    valid = jnp.arange(k_cache.shape[1], dtype=jnp.int32)[None, :] < lengths[:, None]
    valid = valid[:, None, None, :]
    scores = jnp.where(valid, scores, -1e30)
    top = jnp.max(scores, axis=-1, keepdims=True)
    expd = jnp.where(valid, jnp.exp(scores - top), 0.0)
    probs = (expd / jnp.sum(expd, axis=-1, keepdims=True)).astype(jnp.bfloat16)
    mixed = jnp.einsum("rkgl,rlkd->rkgd", probs.astype(jnp.float32), value_cache.astype(jnp.float32))
    return mixed.astype(jnp.bfloat16).reshape(reqs, heads * head_dim)


def reference(tokens, gate_wts, expert_ids, replica, w_gate, w_up, w_down, queries, k_cache, value_cache, lengths):
    phys_slot = jnp.where((replica == 1) & (expert_ids < REPLICAS), expert_ids + EXPERTS, expert_ids).astype(jnp.int32)
    owner_dev = phys_slot // SLOT_DEV
    slot_bit = phys_slot % SLOT_DEV
    gate_values = gate_wts.astype(jnp.float32)
    bound = DEVS_PART * CAP

    def per_device(total, device):
        hits_mask = owner_dev == device
        routed_to = jnp.any(hits_mask, axis=1)
        order = jnp.argsort(jnp.where(routed_to, 0, 1).astype(jnp.int32), stable=True)[:bound].astype(jnp.int32)
        chosen = tokens[order]
        result = jnp.zeros((bound, D), jnp.float32)
        for j in range(SLOT_DEV):
            coefficients = jnp.sum(jnp.where(hits_mask & (slot_bit == j), gate_values, 0.0), axis=1)[order]
            index = device * SLOT_DEV + j
            gated = jnp.dot(chosen, w_gate[index], preferred_element_type=jnp.float32)
            upward = jnp.dot(chosen, w_up[index], preferred_element_type=jnp.float32)
            hidden = (jax.nn.silu(gated) * upward).astype(jnp.bfloat16)
            result = result + coefficients[:, None] * jnp.dot(hidden, w_down[index], preferred_element_type=jnp.float32)
        rounded = lax.optimization_barrier(result.astype(jnp.bfloat16)).astype(jnp.float32)
        return total.at[order].add(rounded), None

    total, _ = lax.scan(per_device, jnp.zeros((TOKENS, D), jnp.float32), jnp.arange(DEVS_PART, dtype=jnp.int32))
    routed_out = total.astype(jnp.bfloat16)
    return routed_out, attend(queries, k_cache, value_cache, lengths)
```

```python
import functools

import jax
import jax.numpy as jnp
from jax import lax
from jax.experimental import pallas as pl
from jax.experimental.pallas import tpu as pltpu
from jax.sharding import PartitionSpec as P

SLOT_DEV = 2
LANES = 128
AXES = ("wide", "narrow")


def attend(queries, k_cache, value_cache, lengths):
    reqs, heads, head_dim = queries.shape
    kv_heads = k_cache.shape[2]
    group = heads // kv_heads
    grouped = queries.reshape(reqs, kv_heads, group, head_dim)
    scores = jnp.einsum(
        "rkgd,rlkd->rkgl", grouped, k_cache, preferred_element_type=jnp.float32
    ) * head_dim ** (-0.5)
    valid = jnp.arange(k_cache.shape[1], dtype=jnp.int32)[None, :] < lengths[:, None]
    valid = valid[:, None, None, :]
    scores = jnp.where(valid, scores, -1e30)
    top = jnp.max(scores, axis=-1, keepdims=True)
    expd = jnp.where(valid, jnp.exp(scores - top), 0.0)
    probs = (expd / jnp.sum(expd, axis=-1, keepdims=True)).astype(jnp.bfloat16)
    mixed = jnp.einsum("rkgl,rlkd->rkgd", probs, value_cache, preferred_element_type=jnp.float32)
    return mixed.astype(jnp.bfloat16).reshape(reqs, heads * head_dim)


def pack_kernel(experts, spares, tokens_ref, gate_ref, ids_ref, replica_ref, out_ref):
    rows, width = tokens_ref.shape
    extra = out_ref.shape[1] - width
    ids = ids_ref[...]
    slots = jnp.where((replica_ref[...] == 1) & (ids < spares), ids + experts, ids)
    weights = gate_ref[...].astype(jnp.float32)
    lane = lax.broadcasted_iota(jnp.int32, (rows, extra), 1)
    coef = jnp.zeros((rows, extra), jnp.float32)
    for k in range(ids.shape[1]):
        coef = coef + jnp.where(lane == slots[:, k : k + 1], weights[:, k : k + 1], 0.0)
    out_ref[:, :width] = tokens_ref[...]
    out_ref[:, width:] = coef.astype(out_ref.dtype)


def pack(tokens, gate_wts, expert_ids, replica, devices):
    rows, width = tokens.shape
    extra = pl.cdiv(SLOT_DEV * devices, LANES) * LANES
    return pl.pallas_call(
        functools.partial(pack_kernel, 3 * devices // 2, devices // 2),
        out_shape=jax.ShapeDtypeStruct((rows, width + extra), tokens.dtype),
        name="pack",
    )(tokens, gate_wts, expert_ids, replica)


def expert_kernel(count, with_sum, first_ref, *refs):
    blocks, refs = refs[:count], refs[count:]
    gate_hbm, up_hbm, down_hbm = refs[:3]
    refs = refs[3:]
    sums, refs = (refs[:count], refs[count:]) if with_sum else ((), refs)
    outs, refs = refs[:count], refs[count:]
    x_ref, gu_ref, down_ref, hidden_ref, x_sem, w_sem = refs
    rows = blocks[0].shape[0]
    slots, width, half = gate_hbm.shape
    x_copies = [
        pltpu.make_async_copy(blocks[i], x_ref.at[pl.ds(i * rows, rows)], x_sem.at[i])
        for i in range(count)
    ]
    w_copies = []
    for j in range(slots):
        w_copies.append(
            pltpu.make_async_copy(gate_hbm.at[j], gu_ref.at[j, :, pl.ds(0, half)], w_sem.at[j, 0])
        )
        w_copies.append(
            pltpu.make_async_copy(up_hbm.at[j], gu_ref.at[j, :, pl.ds(half, half)], w_sem.at[j, 1])
        )
    for j in range(slots):
        w_copies.append(
            pltpu.make_async_copy(down_hbm.at[j], down_ref.at[pl.ds(j * half, half)], w_sem.at[j, 2])
        )
    for copy in x_copies + w_copies:
        copy.start()
    for copy in x_copies:
        copy.wait()
    shares = x_ref[:, width:].astype(jnp.float32)
    lane = lax.broadcasted_iota(jnp.int32, shares.shape, 1)
    for j in range(slots):
        w_copies[2 * j].wait()
        w_copies[2 * j + 1].wait()
        coef = jnp.sum(jnp.where(lane == first_ref[0] + j, shares, 0.0), axis=1, keepdims=True)
        both = jnp.dot(x_ref[:, :width], gu_ref[j], preferred_element_type=jnp.float32)
        gated, upward = both[:, :half], both[:, half:]
        hidden = gated / (1.0 + jnp.exp(-gated)) * upward * coef
        hidden_ref[:, j * half : (j + 1) * half] = hidden.astype(hidden_ref.dtype)
    for j in range(slots):
        w_copies[2 * slots + j].wait()
    result = jnp.dot(hidden_ref[...], down_ref[...], preferred_element_type=jnp.float32)
    for i in range(count):
        part = result[i * rows : (i + 1) * rows]
        if with_sum:
            part = part + sums[i][...]
        outs[i][...] = part.astype(outs[i].dtype)


def expert(blocks, weights, first, sums, dtype):
    w_gate, w_up, w_down = weights
    count = len(blocks)
    rows, packed = blocks[0].shape
    slots, width, half = w_gate.shape
    anywhere = pl.BlockSpec(memory_space=pl.ANY)
    whole = pl.BlockSpec(memory_space=pltpu.VMEM)
    return pl.pallas_call(
        functools.partial(expert_kernel, count, bool(sums)),
        out_shape=[jax.ShapeDtypeStruct((rows, width), dtype)] * count,
        in_specs=[pl.BlockSpec(memory_space=pltpu.SMEM)]
        + [anywhere] * (count + 3)
        + [whole] * len(sums),
        out_specs=[whole] * count,
        scratch_shapes=[
            pltpu.VMEM((count * rows, packed), blocks[0].dtype),
            pltpu.VMEM((slots, width, 2 * half), w_gate.dtype),
            pltpu.VMEM((slots * half, width), w_down.dtype),
            pltpu.VMEM((count * rows, slots * half), blocks[0].dtype),
            pltpu.SemaphoreType.DMA((count,)),
            pltpu.SemaphoreType.DMA((slots, 3)),
        ],
        compiler_params=pltpu.CompilerParams(vmem_limit_bytes=40 << 20),
        name="expert",
    )(first, *blocks, *weights, *sums)


def permutations(chips):
    ring = list(range(0, chips, 2)) + list(range(chips - 1 - chips % 2, 0, -2))
    step = {ring[i]: ring[(i + 1) % chips] for i in range(chips)}
    same = [(2 * a, 2 * b) for a, b in step.items()] + [(2 * b + 1, 2 * a + 1) for a, b in step.items()]
    cross = [(2 * a + 1, 2 * b) for a, b in step.items()] + [(2 * b, 2 * a + 1) for a, b in step.items()]
    return same, cross, [(b, a) for a, b in same], [(b, a) for a, b in cross]


def local(
    tokens,
    gate_wts,
    expert_ids,
    replica,
    w_gate,
    w_up,
    w_down,
    queries,
    k_cache,
    value_cache,
    lengths,
):
    chips = lax.axis_size("wide")
    devices = chips * lax.axis_size("narrow")
    same, cross, same_back, cross_back = permutations(chips)
    far = chips // 2
    own = pack(tokens, gate_wts, expert_ids, replica, devices)
    near_rows, far_rows = {}, {}
    near_rows[1] = lax.ppermute(own, AXES, same)
    far_rows[1] = lax.ppermute(own, AXES, cross)
    mine = (w_gate, w_up, w_down)
    theirs = tuple(lax.ppermute(w, "narrow", [(0, 1), (1, 0)]) for w in mine)
    for k in range(2, far + 1):
        near_rows[k] = lax.ppermute(near_rows[k - 1], AXES, same)
        if k < far:
            far_rows[k] = lax.ppermute(far_rows[k - 1], AXES, same)
    me = lax.axis_index("wide") * 2 + lax.axis_index("narrow")
    my_first = (me * SLOT_DEV).astype(jnp.int32).reshape(1)
    their_first = ((me + 1 - 2 * lax.axis_index("narrow")) * SLOT_DEV).astype(jnp.int32).reshape(1)
    groups = []
    top = far
    while top > 2:
        groups.append([top - 1, top])
        top -= 2
    groups.append(list(range(0, top + 1)))
    partial = {}
    for group in reversed(groups):
        names, blocks = [], []
        for k in group:
            if k == 0:
                names.append(("own", 0))
                blocks.append(own)
                continue
            names.append(("near", k))
            blocks.append(near_rows[k])
            if k < far:
                names.append(("far", k))
                blocks.append(far_rows[k])
        sums = expert(blocks, mine, my_first, [], jnp.float32)
        outs = expert(blocks, theirs, their_first, sums, jnp.bfloat16)
        partial.update(zip(names, outs, strict=True))
    near_sum = partial["near", far]
    far_sum = partial["far", far - 1]
    for k in range(far - 1, 0, -1):
        near_sum = lax.ppermute(near_sum, AXES, same_back)
        near_sum = (near_sum.astype(jnp.float32) + partial["near", k].astype(jnp.float32)).astype(jnp.bfloat16)
        if k < far - 1:
            far_sum = lax.ppermute(far_sum, AXES, same_back)
            far_sum = (far_sum.astype(jnp.float32) + partial["far", k].astype(jnp.float32)).astype(jnp.bfloat16)
    near_sum = lax.ppermute(near_sum, AXES, same_back)
    far_sum = lax.ppermute(far_sum, AXES, cross_back)
    attn_out = attend(queries, k_cache, value_cache, lengths)
    routed_out = (
        near_sum.astype(jnp.float32)
        + far_sum.astype(jnp.float32)
        + partial["own", 0].astype(jnp.float32)
    ).astype(jnp.bfloat16)
    return (routed_out, attn_out)


def solution(mesh):
    rows = P(("groups", "wide", "narrow"))
    slots = P(("wide", "narrow"))
    in_specs = (rows, rows, rows, rows, slots, slots, slots, rows, rows, rows, rows)
    return jax.shard_map(local, mesh=mesh, in_specs=in_specs, out_specs=(rows, rows), check_vma=False)
```

```python
import functools

import jax
import jax.numpy as jnp
from jax import lax
from jax.experimental import pallas as pl
from jax.experimental.pallas import tpu as pltpu
from jax.sharding import PartitionSpec as P


SLOT_DEV = 2
LANES = 128
AXES = ("wide", "narrow")
VMEM_LIMIT = 24 << 20


def attend(queries, k_cache, value_cache, lengths):
    reqs, heads, head_dim = queries.shape
    kv_heads = k_cache.shape[2]
    group = heads // kv_heads
    grouped = queries.reshape(reqs, kv_heads, group, head_dim)
    scores = jnp.einsum(
        "rkgd,rlkd->rkgl", grouped, k_cache, preferred_element_type=jnp.float32
    ) * head_dim ** (-0.5)
    valid = jnp.arange(k_cache.shape[1], dtype=jnp.int32)[None, :] < lengths[:, None]
    valid = valid[:, None, None, :]
    scores = jnp.where(valid, scores, -1e30)
    top = jnp.max(scores, axis=-1, keepdims=True)
    expd = jnp.where(valid, jnp.exp(scores - top), 0.0)
    probs = (expd / jnp.sum(expd, axis=-1, keepdims=True)).astype(jnp.bfloat16)
    mixed = jnp.einsum("rkgl,rlkd->rkgd", probs, value_cache, preferred_element_type=jnp.float32)
    return mixed.astype(jnp.bfloat16).reshape(reqs, heads * head_dim)


def pack_kernel(experts, spares, tokens_ref, gate_ref, ids_ref, replica_ref, out_ref):
    rows, width = tokens_ref.shape
    extra = out_ref.shape[1] - width
    ids = ids_ref[...]
    slots = jnp.where((replica_ref[...] == 1) & (ids < spares), ids + experts, ids)
    weights = gate_ref[...].astype(jnp.float32)
    slot = lax.broadcasted_iota(jnp.int32, (extra, rows), 0)
    coef = jnp.zeros((extra, rows), jnp.float32)
    for k in range(ids.shape[0]):
        coef = coef + jnp.where(slot == slots[k : k + 1, :], weights[k : k + 1, :], 0.0)
    out_ref[:, :width] = tokens_ref[...]
    out_ref[:, width:] = coef.T.astype(out_ref.dtype)


def pack(tokens, gate_wts, expert_ids, replica, devices):
    rows, width = tokens.shape
    extra = pl.cdiv(SLOT_DEV * devices, LANES) * LANES
    return pl.pallas_call(
        functools.partial(pack_kernel, 3 * devices // 2, devices // 2),
        out_shape=jax.ShapeDtypeStruct((rows, width + extra), tokens.dtype),
        name="pack",
    )(tokens, gate_wts.T, expert_ids.T, replica.T)


def stage_kernel(first_ref, gate, up, down, gu_ref, down_ref, sem):
    slots, _, half = gate.shape
    copies = []
    for j in range(slots):
        copies.append(pltpu.make_async_copy(gate.at[j], gu_ref.at[j, :, pl.ds(0, half)], sem.at[j, 0]))
        copies.append(pltpu.make_async_copy(up.at[j], gu_ref.at[j, :, pl.ds(half, half)], sem.at[j, 1]))
        copies.append(pltpu.make_async_copy(down.at[j], down_ref.at[j], sem.at[j, 2]))
    for copy in copies:
        copy.start()
    for copy in copies:
        copy.wait()


def stage(first, gate, up, down):
    slots, width, half = gate.shape
    anywhere = pl.BlockSpec(memory_space=pl.ANY)
    return pl.pallas_call(
        stage_kernel,
        out_shape=[
            pltpu.VMEM((slots, width, 2 * half), gate.dtype),
            pltpu.VMEM((slots, half, width), down.dtype),
        ],
        in_specs=[pl.BlockSpec(memory_space=pltpu.SMEM)] + [anywhere] * 3,
        out_specs=[anywhere] * 2,
        scratch_shapes=[pltpu.SemaphoreType.DMA((slots, 3))],
        compiler_params=pltpu.CompilerParams(vmem_limit_bytes=4 << 20),
        name="stage",
    )(first, *(pltpu.with_memory_space_constraint(w, pltpu.HBM) for w in (gate, up, down)))


def expert_kernel(count, sources, base, with_sum, first_ref, *refs):
    blocks, refs = refs[:count], refs[count:]
    weights, refs = refs[: 2 * sources], refs[2 * sources :]
    sums, refs = (refs[:count], refs[count:]) if with_sum else ((), refs)
    outs, refs = refs[:count], refs[count:]
    x_ref, hidden_ref, x_sem = refs
    rows = blocks[0].shape[0]
    slots, half, width = weights[1].shape
    copies = [
        pltpu.make_async_copy(blocks[i], x_ref.at[pl.ds(i * rows, rows)], x_sem.at[i])
        for i in range(count)
    ]
    for copy in copies:
        copy.start()
    for copy in copies:
        copy.wait()
    shares = x_ref[:, width:].astype(jnp.float32)
    lane = lax.broadcasted_iota(jnp.int32, shares.shape, 1)
    result = None
    for n in range(sources):
        gu_ref, down_ref = weights[2 * n : 2 * n + 2]
        for j in range(slots):
            coef = jnp.sum(jnp.where(lane == first_ref[base + n] + j, shares, 0.0), axis=1, keepdims=True)
            both = jnp.dot(x_ref[:, :width], gu_ref[j], preferred_element_type=jnp.float32)
            gated, upward = both[:, :half], both[:, half:]
            hidden = gated / (1.0 + jnp.exp(-gated)) * upward * coef
            hidden_ref[:, j * half : (j + 1) * half] = hidden.astype(hidden_ref.dtype)
        down = down_ref[...].reshape(slots * half, width)
        part = jnp.dot(hidden_ref[...], down, preferred_element_type=jnp.float32)
        result = part if result is None else result + part
    for i in range(count):
        part = result[i * rows : (i + 1) * rows]
        if with_sum:
            part = part + sums[i][...]
        outs[i][...] = part.astype(outs[i].dtype)


def expert(blocks, weights, base, first, sums, dtype):
    count = len(blocks)
    sources = len(weights) // 2
    rows, packed = blocks[0].shape
    slots, half, width = weights[1].shape
    anywhere = pl.BlockSpec(memory_space=pl.ANY)
    whole = pl.BlockSpec(memory_space=pltpu.VMEM)
    weights = [pltpu.with_memory_space_constraint(w, pltpu.VMEM) for w in weights]
    return pl.pallas_call(
        functools.partial(expert_kernel, count, sources, base, bool(sums)),
        out_shape=[jax.ShapeDtypeStruct((rows, width), dtype)] * count,
        in_specs=[pl.BlockSpec(memory_space=pltpu.SMEM)]
        + [anywhere] * count
        + [whole] * (len(weights) + len(sums)),
        out_specs=[whole] * count,
        scratch_shapes=[
            pltpu.VMEM((count * rows, packed), blocks[0].dtype),
            pltpu.VMEM((count * rows, slots * half), blocks[0].dtype),
            pltpu.SemaphoreType.DMA((count,)),
        ],
        compiler_params=pltpu.CompilerParams(vmem_limit_bytes=VMEM_LIMIT),
        name="expert",
    )(first, *blocks, *weights, *sums)


def permutations(chips):
    ring = list(range(0, chips, 2)) + list(range(chips - 1 - chips % 2, 0, -2))
    step = {ring[i]: ring[(i + 1) % chips] for i in range(chips)}
    same = [(2 * a, 2 * b) for a, b in step.items()] + [(2 * b + 1, 2 * a + 1) for a, b in step.items()]
    cross = [(2 * a + 1, 2 * b) for a, b in step.items()] + [(2 * b, 2 * a + 1) for a, b in step.items()]
    return same, cross, [(b, a) for a, b in same], [(b, a) for a, b in cross]


def local(
    tokens,
    gate_wts,
    expert_ids,
    replica,
    w_gate,
    w_up,
    w_down,
    queries,
    k_cache,
    value_cache,
    lengths,
):
    chips = lax.axis_size("wide")
    devices = chips * lax.axis_size("narrow")
    same, cross, same_back, cross_back = permutations(chips)
    far = chips // 2
    core = lax.axis_index("narrow")
    me = lax.axis_index("wide") * 2 + core
    mine_first = me * SLOT_DEV
    theirs_first = (me + 1 - 2 * core) * SLOT_DEV
    first = jnp.stack([mine_first, theirs_first]).astype(jnp.int32)
    own = pack(tokens, gate_wts, expert_ids, replica, devices)
    near_rows, far_rows = {}, {}
    near_rows[1] = lax.ppermute(own, AXES, same)
    far_rows[1] = lax.ppermute(own, AXES, cross)
    swapped = []
    for w in (w_gate, w_up, w_down):
        swapped.append(lax.ppermute(w, "narrow", [(0, 1), (1, 0)]))
    mine = list(stage(first, w_gate, w_up, w_down))
    theirs = list(stage(first, *swapped))
    for k in range(2, far + 1):
        near_rows[k] = lax.ppermute(near_rows[k - 1], AXES, same)
        if k < far:
            far_rows[k] = lax.ppermute(far_rows[k - 1], AXES, same)
    partial = {}
    for group in groups_of(far):
        names, blocks = [], []
        for k in group:
            if k == 0:
                names.append(("own", 0))
                blocks.append(own)
                continue
            names.append(("near", k))
            blocks.append(near_rows[k])
            if k < far:
                names.append(("far", k))
                blocks.append(far_rows[k])
        top = group[-1]
        if top == far:
            outs = expert(blocks, mine + theirs, 0, first, [], jnp.bfloat16)
        else:
            sums = expert(blocks, mine, 0, first, [], jnp.float32)
            outs = expert(blocks, theirs, 1, first, sums, jnp.bfloat16)
        partial.update(zip(names, outs, strict=True))
    near_sum = partial["near", far]
    far_sum = partial["far", far - 1]
    for k in range(far - 1, 0, -1):
        near_sum = lax.ppermute(near_sum, AXES, same_back)
        near_sum = add(near_sum, partial["near", k])
        if k < far - 1:
            far_sum = lax.ppermute(far_sum, AXES, same_back)
            far_sum = add(far_sum, partial["far", k])
    near_sum = lax.ppermute(near_sum, AXES, same_back)
    far_sum = lax.ppermute(far_sum, AXES, cross_back)
    lengths, own_part = lax.optimization_barrier((lengths, partial["own", 0]))
    attn_out = attend(queries, k_cache, value_cache, lengths)
    routed_out = add(near_sum, far_sum, own_part)
    return (routed_out, attn_out)


def add(*values):
    return sum(v.astype(jnp.float32) for v in values).astype(jnp.bfloat16)


def groups_of(far):
    groups = []
    while far > 2:
        groups.append([far - 1, far])
        far -= 2
    groups.append(list(range(far + 1)))
    return groups[::-1]


def solution(mesh):
    rows = P(("groups", "wide", "narrow"))
    slots = P(("wide", "narrow"))
    in_specs = (rows, rows, rows, rows, slots, slots, slots, rows, rows, rows, rows)
    return jax.shard_map(local, mesh=mesh, in_specs=in_specs, out_specs=(rows, rows), check_vma=False)
```

```python
import functools

import jax
import jax.numpy as jnp
from jax import lax
from jax.experimental import pallas as pl
from jax.experimental.pallas import tpu as pltpu
from jax.sharding import PartitionSpec as P


SLOT_DEV = 2
LANES = 128
AXES = ("wide", "narrow")
VMEM_LIMIT = 24 << 20


def attend(queries, k_cache, value_cache, lengths):
    reqs, heads, head_dim = queries.shape
    kv_heads = k_cache.shape[2]
    group = heads // kv_heads
    grouped = queries.reshape(reqs, kv_heads, group, head_dim)
    scores = jnp.einsum(
        "rkgd,rlkd->rkgl", grouped, k_cache, preferred_element_type=jnp.float32
    ) * head_dim ** (-0.5)
    valid = jnp.arange(k_cache.shape[1], dtype=jnp.int32)[None, :] < lengths[:, None]
    valid = valid[:, None, None, :]
    scores = jnp.where(valid, scores, -1e30)
    top = jnp.max(scores, axis=-1, keepdims=True)
    expd = jnp.where(valid, jnp.exp(scores - top), 0.0)
    probs = (expd / jnp.sum(expd, axis=-1, keepdims=True)).astype(jnp.bfloat16)
    mixed = jnp.einsum("rkgl,rlkd->rkgd", probs, value_cache, preferred_element_type=jnp.float32)
    return mixed.astype(jnp.bfloat16).reshape(reqs, heads * head_dim)


def pack_kernel(experts, spares, tokens, gate, ids, replica, out_ref, gate_ref, ids_ref, replica_ref, sem):
    rows, width = tokens.shape
    extra = out_ref.shape[1] - width
    copies = [
        pltpu.make_async_copy(gate, gate_ref, sem.at[0]),
        pltpu.make_async_copy(ids, ids_ref, sem.at[1]),
        pltpu.make_async_copy(replica, replica_ref, sem.at[2]),
        pltpu.make_async_copy(tokens, out_ref.at[:, pl.ds(0, width)], sem.at[3]),
    ]
    for copy in copies:
        copy.start()
    for copy in copies[:3]:
        copy.wait()
    slots = jnp.where(
        (replica_ref[...] == 1) & (ids_ref[...] < spares), ids_ref[...] + experts, ids_ref[...]
    )
    weights = gate_ref[...].astype(jnp.float32)
    slot = lax.broadcasted_iota(jnp.int32, (extra, rows), 0)
    coef = jnp.zeros((extra, rows), jnp.float32)
    for k in range(slots.shape[0]):
        coef = coef + jnp.where(slot == slots[k : k + 1, :], weights[k : k + 1, :], 0.0)
    out_ref[:, width:] = coef.T.astype(out_ref.dtype)
    copies[3].wait()


def pack(tokens, gate_wts, expert_ids, replica, devices):
    rows, width = tokens.shape
    top_count = gate_wts.shape[1]
    extra = pl.cdiv(SLOT_DEV * devices, LANES) * LANES
    return pl.pallas_call(
        functools.partial(pack_kernel, 3 * devices // 2, devices // 2),
        out_shape=jax.ShapeDtypeStruct((rows, width + extra), tokens.dtype),
        in_specs=[pl.BlockSpec(memory_space=pl.ANY)] * 4,
        out_specs=pl.BlockSpec(memory_space=pltpu.VMEM),
        scratch_shapes=[
            pltpu.VMEM((top_count, rows), gate_wts.dtype),
            pltpu.VMEM((top_count, rows), expert_ids.dtype),
            pltpu.VMEM((top_count, rows), replica.dtype),
            pltpu.SemaphoreType.DMA((4,)),
        ],
        compiler_params=pltpu.CompilerParams(vmem_limit_bytes=4 << 20),
        name="pack",
    )(*(pltpu.with_memory_space_constraint(v, pltpu.HBM) for v in (tokens, gate_wts.T, expert_ids.T, replica.T)))


def stage_kernel(first_ref, gate, up, down, gu_ref, down_ref, sem):
    slots, _, half = gate.shape
    copies = []
    for j in range(slots):
        copies.append(pltpu.make_async_copy(gate.at[j], gu_ref.at[j, :, pl.ds(0, half)], sem.at[j, 0]))
        copies.append(pltpu.make_async_copy(up.at[j], gu_ref.at[j, :, pl.ds(half, half)], sem.at[j, 1]))
        copies.append(pltpu.make_async_copy(down.at[j], down_ref.at[j], sem.at[j, 2]))
    for copy in copies:
        copy.start()
    for copy in copies:
        copy.wait()


def stage(first, gate, up, down):
    slots, width, half = gate.shape
    anywhere = pl.BlockSpec(memory_space=pl.ANY)
    return pl.pallas_call(
        stage_kernel,
        out_shape=[
            pltpu.VMEM((slots, width, 2 * half), gate.dtype),
            pltpu.VMEM((slots, half, width), down.dtype),
        ],
        in_specs=[pl.BlockSpec(memory_space=pltpu.SMEM)] + [anywhere] * 3,
        out_specs=[anywhere] * 2,
        scratch_shapes=[pltpu.SemaphoreType.DMA((slots, 3))],
        compiler_params=pltpu.CompilerParams(vmem_limit_bytes=4 << 20),
        name="stage",
    )(first, *(pltpu.with_memory_space_constraint(w, pltpu.HBM) for w in (gate, up, down)))


def expert_kernel(count, sources, base, with_sum, first_ref, *refs):
    blocks, refs = refs[:count], refs[count:]
    weights, refs = refs[: 2 * sources], refs[2 * sources :]
    sums, refs = (refs[:count], refs[count:]) if with_sum else ((), refs)
    outs, refs = refs[:count], refs[count:]
    x_ref, hidden_ref, x_sem = refs
    rows = blocks[0].shape[0]
    slots, half, width = weights[1].shape
    copies = [
        pltpu.make_async_copy(blocks[i], x_ref.at[pl.ds(i * rows, rows)], x_sem.at[i])
        for i in range(count)
    ]
    for copy in copies:
        copy.start()
    for copy in copies:
        copy.wait()
    shares = x_ref[:, width:].astype(jnp.float32)
    lane = lax.broadcasted_iota(jnp.int32, shares.shape, 1)
    result = None
    for n in range(sources):
        gu_ref, down_ref = weights[2 * n : 2 * n + 2]
        for j in range(slots):
            coef = jnp.sum(jnp.where(lane == first_ref[base + n] + j, shares, 0.0), axis=1, keepdims=True)
            both = jnp.dot(x_ref[:, :width], gu_ref[j], preferred_element_type=jnp.float32)
            gated, upward = both[:, :half], both[:, half:]
            hidden = gated / (1.0 + jnp.exp(-gated)) * upward * coef
            hidden_ref[:, j * half : (j + 1) * half] = hidden.astype(hidden_ref.dtype)
        down = down_ref[...].reshape(slots * half, width)
        part = jnp.dot(hidden_ref[...], down, preferred_element_type=jnp.float32)
        result = part if result is None else result + part
    for i in range(count):
        part = result[i * rows : (i + 1) * rows]
        if with_sum:
            part = part + sums[i][...]
        outs[i][...] = part.astype(outs[i].dtype)


def expert(blocks, weights, base, first, sums, dtype):
    count = len(blocks)
    sources = len(weights) // 2
    rows, packed = blocks[0].shape
    slots, half, width = weights[1].shape
    anywhere = pl.BlockSpec(memory_space=pl.ANY)
    whole = pl.BlockSpec(memory_space=pltpu.VMEM)
    weights = [pltpu.with_memory_space_constraint(w, pltpu.VMEM) for w in weights]
    return pl.pallas_call(
        functools.partial(expert_kernel, count, sources, base, bool(sums)),
        out_shape=[jax.ShapeDtypeStruct((rows, width), dtype)] * count,
        in_specs=[pl.BlockSpec(memory_space=pltpu.SMEM)]
        + [anywhere] * count
        + [whole] * (len(weights) + len(sums)),
        out_specs=[whole] * count,
        scratch_shapes=[
            pltpu.VMEM((count * rows, packed), blocks[0].dtype),
            pltpu.VMEM((count * rows, slots * half), blocks[0].dtype),
            pltpu.SemaphoreType.DMA((count,)),
        ],
        compiler_params=pltpu.CompilerParams(vmem_limit_bytes=VMEM_LIMIT),
        name="expert",
    )(first, *blocks, *weights, *sums)


def permutations(chips):
    ring = list(range(0, chips, 2)) + list(range(chips - 1 - chips % 2, 0, -2))
    step = {ring[i]: ring[(i + 1) % chips] for i in range(chips)}
    same = [(2 * a, 2 * b) for a, b in step.items()] + [(2 * b + 1, 2 * a + 1) for a, b in step.items()]
    cross = [(2 * a + 1, 2 * b) for a, b in step.items()] + [(2 * b, 2 * a + 1) for a, b in step.items()]
    return same, cross, [(b, a) for a, b in same], [(b, a) for a, b in cross]


def local(
    tokens,
    gate_wts,
    expert_ids,
    replica,
    w_gate,
    w_up,
    w_down,
    queries,
    k_cache,
    value_cache,
    lengths,
):
    chips = lax.axis_size("wide")
    devices = chips * lax.axis_size("narrow")
    same, cross, same_back, cross_back = permutations(chips)
    far = chips // 2
    core = lax.axis_index("narrow")
    me = lax.axis_index("wide") * 2 + core
    mine_first = me * SLOT_DEV
    theirs_first = (me + 1 - 2 * core) * SLOT_DEV
    first = jnp.stack([mine_first, theirs_first]).astype(jnp.int32)
    own = pack(tokens, gate_wts, expert_ids, replica, devices)
    near_rows, far_rows = {}, {}
    near_rows[1] = lax.ppermute(own, AXES, same)
    far_rows[1] = lax.ppermute(own, AXES, cross)
    mine = list(stage(first, w_gate, w_up, w_down))
    theirs = []
    for w in mine:
        theirs.append(lax.ppermute(w, "narrow", [(0, 1), (1, 0)]))
    for k in range(2, far + 1):
        near_rows[k] = lax.ppermute(near_rows[k - 1], AXES, same)
        if k < far:
            far_rows[k] = lax.ppermute(far_rows[k - 1], AXES, same)
    partial = {}
    for group in groups_of(far):
        names, blocks = [], []
        for k in group:
            if k == 0:
                names.append(("own", 0))
                blocks.append(own)
                continue
            names.append(("near", k))
            blocks.append(near_rows[k])
            if k < far:
                names.append(("far", k))
                blocks.append(far_rows[k])
        top = group[-1]
        if top == far:
            outs = expert(blocks, mine + theirs, 0, first, [], jnp.bfloat16)
        else:
            sums = expert(blocks, mine, 0, first, [], jnp.float32)
            outs = expert(blocks, theirs, 1, first, sums, jnp.bfloat16)
        partial.update(zip(names, outs, strict=True))
    near_sum = partial["near", far]
    far_sum = partial["far", far - 1]
    for k in range(far - 1, 0, -1):
        near_sum = lax.ppermute(near_sum, AXES, same_back)
        near_sum = add(near_sum, partial["near", k])
        if k < far - 1:
            far_sum = lax.ppermute(far_sum, AXES, same_back)
            far_sum = add(far_sum, partial["far", k])
    lengths, near_sum = lax.optimization_barrier((lengths, near_sum))
    near_sum = lax.ppermute(near_sum, AXES, same_back)
    far_sum = lax.ppermute(far_sum, AXES, cross_back)
    attn_out = attend(queries, k_cache, value_cache, lengths)
    routed_out = add(near_sum, far_sum, partial["own", 0])
    return (routed_out, attn_out)


def add(*values):
    return sum(v.astype(jnp.float32) for v in values).astype(jnp.bfloat16)


def groups_of(far):
    groups = []
    while far > 2:
        groups.append([far - 1, far])
        far -= 2
    groups.append(list(range(far + 1)))
    return groups[::-1]


def solution(mesh):
    rows = P(("groups", "wide", "narrow"))
    slots = P(("wide", "narrow"))
    in_specs = (rows, rows, rows, rows, slots, slots, slots, rows, rows, rows, rows)
    return jax.shard_map(local, mesh=mesh, in_specs=in_specs, out_specs=(rows, rows), check_vma=False)
```

```python
import functools

import jax
import jax.numpy as jnp
from jax import lax
from jax.experimental import pallas as pl
from jax.experimental.pallas import tpu as pltpu
from jax.sharding import PartitionSpec as P


SLOT_DEV = 2
LANES = 128
AXES = ("wide", "narrow")
VMEM_LIMIT = 24 << 20


def attend(queries, k_cache, value_cache, lengths):
    reqs, heads, head_dim = queries.shape
    kv_heads = k_cache.shape[2]
    group = heads // kv_heads
    grouped = queries.reshape(reqs, kv_heads, group, head_dim)
    scores = jnp.einsum(
        "rkgd,rlkd->rkgl", grouped, k_cache, preferred_element_type=jnp.float32
    ) * head_dim ** (-0.5)
    valid = jnp.arange(k_cache.shape[1], dtype=jnp.int32)[None, :] < lengths[:, None]
    valid = valid[:, None, None, :]
    scores = jnp.where(valid, scores, -1e30)
    top = jnp.max(scores, axis=-1, keepdims=True)
    expd = jnp.where(valid, jnp.exp(scores - top), 0.0)
    probs = (expd / jnp.sum(expd, axis=-1, keepdims=True)).astype(jnp.bfloat16)
    mixed = jnp.einsum("rkgl,rlkd->rkgd", probs, value_cache, preferred_element_type=jnp.float32)
    return mixed.astype(jnp.bfloat16).reshape(reqs, heads * head_dim)


def pack_kernel(experts, spares, tokens, gate, ids, replica, out_ref, gate_ref, ids_ref, replica_ref, sem):
    rows, width = tokens.shape
    extra = out_ref.shape[1] - width
    copies = [
        pltpu.make_async_copy(gate, gate_ref, sem.at[0]),
        pltpu.make_async_copy(ids, ids_ref, sem.at[1]),
        pltpu.make_async_copy(replica, replica_ref, sem.at[2]),
        pltpu.make_async_copy(tokens, out_ref.at[:, pl.ds(0, width)], sem.at[3]),
    ]
    for copy in copies:
        copy.start()
    for copy in copies[:3]:
        copy.wait()
    slots = jnp.where(
        (replica_ref[...] == 1) & (ids_ref[...] < spares), ids_ref[...] + experts, ids_ref[...]
    )
    weights = gate_ref[...].astype(jnp.float32)
    slot = lax.broadcasted_iota(jnp.int32, (extra, rows), 0)
    coef = jnp.zeros((extra, rows), jnp.float32)
    for k in range(slots.shape[0]):
        coef = coef + jnp.where(slot == slots[k : k + 1, :], weights[k : k + 1, :], 0.0)
    out_ref[:, width:] = coef.T.astype(out_ref.dtype)
    copies[3].wait()


def pack(tokens, gate_wts, expert_ids, replica, devices):
    rows, width = tokens.shape
    top_count = gate_wts.shape[1]
    extra = pl.cdiv(SLOT_DEV * devices, LANES) * LANES
    return pl.pallas_call(
        functools.partial(pack_kernel, 3 * devices // 2, devices // 2),
        out_shape=jax.ShapeDtypeStruct((rows, width + extra), tokens.dtype),
        in_specs=[pl.BlockSpec(memory_space=pl.ANY)] * 4,
        out_specs=pl.BlockSpec(memory_space=pltpu.VMEM),
        scratch_shapes=[
            pltpu.VMEM((top_count, rows), gate_wts.dtype),
            pltpu.VMEM((top_count, rows), expert_ids.dtype),
            pltpu.VMEM((top_count, rows), replica.dtype),
            pltpu.SemaphoreType.DMA((4,)),
        ],
        compiler_params=pltpu.CompilerParams(vmem_limit_bytes=4 << 20),
        name="pack",
    )(*(pltpu.with_memory_space_constraint(v, pltpu.HBM) for v in (tokens, gate_wts.T, expert_ids.T, replica.T)))


def stage_kernel(first_ref, gate, up, down, gu_ref, down_ref, sem):
    slots, _, half = gate.shape
    copies = []
    for j in range(slots):
        copies.append(pltpu.make_async_copy(gate.at[j], gu_ref.at[j, :, pl.ds(0, half)], sem.at[j, 0]))
        copies.append(pltpu.make_async_copy(up.at[j], gu_ref.at[j, :, pl.ds(half, half)], sem.at[j, 1]))
        copies.append(pltpu.make_async_copy(down.at[j], down_ref.at[j], sem.at[j, 2]))
    for copy in copies:
        copy.start()
    for copy in copies:
        copy.wait()


def stage(first, gate, up, down):
    slots, width, half = gate.shape
    anywhere = pl.BlockSpec(memory_space=pl.ANY)
    return pl.pallas_call(
        stage_kernel,
        out_shape=[
            pltpu.VMEM((slots, width, 2 * half), gate.dtype),
            pltpu.VMEM((slots, half, width), down.dtype),
        ],
        in_specs=[pl.BlockSpec(memory_space=pltpu.SMEM)] + [anywhere] * 3,
        out_specs=[anywhere] * 2,
        scratch_shapes=[pltpu.SemaphoreType.DMA((slots, 3))],
        compiler_params=pltpu.CompilerParams(vmem_limit_bytes=4 << 20),
        name="stage",
    )(first, *(pltpu.with_memory_space_constraint(w, pltpu.HBM) for w in (gate, up, down)))


def expert_kernel(count, sources, base, with_sum, first_ref, *refs):
    blocks, refs = refs[:count], refs[count:]
    weights, refs = refs[: 2 * sources], refs[2 * sources :]
    sums, refs = (refs[:count], refs[count:]) if with_sum else ((), refs)
    outs, refs = refs[:count], refs[count:]
    x_ref, hidden_ref, x_sem = refs
    rows = blocks[0].shape[0]
    slots, half, width = weights[1].shape
    copies = [
        pltpu.make_async_copy(blocks[i], x_ref.at[pl.ds(i * rows, rows)], x_sem.at[i])
        for i in range(count)
    ]
    for copy in copies:
        copy.start()
    for copy in copies:
        copy.wait()
    shares = x_ref[:, width:].astype(jnp.float32)
    lane = lax.broadcasted_iota(jnp.int32, shares.shape, 1)
    result = None
    for n in range(sources):
        gu_ref, down_ref = weights[2 * n : 2 * n + 2]
        for j in range(slots):
            coef = jnp.sum(jnp.where(lane == first_ref[base + n] + j, shares, 0.0), axis=1, keepdims=True)
            both = jnp.dot(x_ref[:, :width], gu_ref[j], preferred_element_type=jnp.float32)
            gated, upward = both[:, :half], both[:, half:]
            hidden = gated / (1.0 + jnp.exp(-gated)) * upward * coef
            hidden_ref[:, j * half : (j + 1) * half] = hidden.astype(hidden_ref.dtype)
        down = down_ref[...].reshape(slots * half, width)
        part = jnp.dot(hidden_ref[...], down, preferred_element_type=jnp.float32)
        result = part if result is None else result + part
    for i in range(count):
        part = result[i * rows : (i + 1) * rows]
        if with_sum:
            part = part + sums[i][...]
        outs[i][...] = part.astype(outs[i].dtype)


def expert(blocks, weights, base, first, sums, dtype):
    count = len(blocks)
    sources = len(weights) // 2
    rows, packed = blocks[0].shape
    slots, half, width = weights[1].shape
    anywhere = pl.BlockSpec(memory_space=pl.ANY)
    whole = pl.BlockSpec(memory_space=pltpu.VMEM)
    weights = [pltpu.with_memory_space_constraint(w, pltpu.VMEM) for w in weights]
    return pl.pallas_call(
        functools.partial(expert_kernel, count, sources, base, bool(sums)),
        out_shape=[jax.ShapeDtypeStruct((rows, width), dtype)] * count,
        in_specs=[pl.BlockSpec(memory_space=pltpu.SMEM)]
        + [anywhere] * count
        + [whole] * (len(weights) + len(sums)),
        out_specs=[whole] * count,
        scratch_shapes=[
            pltpu.VMEM((count * rows, packed), blocks[0].dtype),
            pltpu.VMEM((count * rows, slots * half), blocks[0].dtype),
            pltpu.SemaphoreType.DMA((count,)),
        ],
        compiler_params=pltpu.CompilerParams(vmem_limit_bytes=VMEM_LIMIT),
        name="expert",
    )(first, *blocks, *weights, *sums)


def permutations(chips):
    ring = list(range(0, chips, 2)) + list(range(chips - 1 - chips % 2, 0, -2))
    ups = [2 * chip + place % 2 for place, chip in enumerate(ring)]
    downs = [2 * chip + (place + 1) % 2 for place, chip in enumerate(ring)]
    same, cross = [], []
    for place in range(chips):
        after = (place + 1) % chips
        same += [(ups[place], ups[after]), (downs[after], downs[place])]
        cross += [(downs[place], ups[after]), (ups[after], downs[place])]
    return same, cross, [(b, a) for a, b in same], [(b, a) for a, b in cross]


def local(
    tokens,
    gate_wts,
    expert_ids,
    replica,
    w_gate,
    w_up,
    w_down,
    queries,
    k_cache,
    value_cache,
    lengths,
):
    chips = lax.axis_size("wide")
    devices = chips * lax.axis_size("narrow")
    same, cross, same_back, cross_back = permutations(chips)
    far = chips // 2
    core = lax.axis_index("narrow")
    me = lax.axis_index("wide") * 2 + core
    mine_first = me * SLOT_DEV
    theirs_first = (me + 1 - 2 * core) * SLOT_DEV
    first = jnp.stack([mine_first, theirs_first]).astype(jnp.int32)
    own = pack(tokens, gate_wts, expert_ids, replica, devices)
    near_rows, far_rows = {}, {}
    near_rows[1] = lax.ppermute(own, AXES, same)
    far_rows[1] = lax.ppermute(own, AXES, cross)
    mine = list(stage(first, w_gate, w_up, w_down))
    theirs = []
    for w in mine:
        theirs.append(lax.ppermute(w, "narrow", [(0, 1), (1, 0)]))
    for k in range(2, far + 1):
        near_rows[k] = lax.ppermute(near_rows[k - 1], AXES, same)
        if k < far:
            far_rows[k] = lax.ppermute(far_rows[k - 1], AXES, same)
    partial = {}
    for group in groups_of(far):
        names, blocks = [], []
        for k in group:
            if k == 0:
                names.append(("own", 0))
                blocks.append(own)
                continue
            names.append(("near", k))
            blocks.append(near_rows[k])
            if k < far:
                names.append(("far", k))
                blocks.append(far_rows[k])
        top = group[-1]
        if top == far:
            outs = expert(blocks, mine + theirs, 0, first, [], jnp.bfloat16)
        else:
            sums = expert(blocks, mine, 0, first, [], jnp.float32)
            outs = expert(blocks, theirs, 1, first, sums, jnp.bfloat16)
        partial.update(zip(names, outs, strict=True))
    near_sum = partial["near", far]
    far_sum = partial["far", far - 1]
    for k in range(far - 1, 0, -1):
        near_sum = lax.ppermute(near_sum, AXES, same_back)
        near_sum = add(near_sum, partial["near", k])
        if k < far - 1:
            far_sum = lax.ppermute(far_sum, AXES, same_back)
            far_sum = add(far_sum, partial["far", k])
    lengths, near_sum = lax.optimization_barrier((lengths, near_sum))
    near_sum = lax.ppermute(near_sum, AXES, same_back)
    far_sum = lax.ppermute(far_sum, AXES, cross_back)
    attn_out = attend(queries, k_cache, value_cache, lengths)
    routed_out = add(near_sum, far_sum, partial["own", 0])
    return (routed_out, attn_out)


def add(*values):
    return sum(v.astype(jnp.float32) for v in values).astype(jnp.bfloat16)


def groups_of(far):
    groups = []
    while far > 2:
        groups.append([far - 1, far])
        far -= 2
    groups.append(list(range(far + 1)))
    return groups[::-1]


def solution(mesh):
    rows = P(("groups", "wide", "narrow"))
    slots = P(("wide", "narrow"))
    in_specs = (rows, rows, rows, rows, slots, slots, slots, rows, rows, rows, rows)
    return jax.shard_map(local, mesh=mesh, in_specs=in_specs, out_specs=(rows, rows), check_vma=False)
```

```python
import functools

import jax
import jax.numpy as jnp
from jax import lax
from jax.experimental import pallas as pl
from jax.experimental.pallas import tpu as pltpu
from jax.sharding import PartitionSpec as P


SLOT_DEV = 2
LANES = 128
AXES = ("wide", "narrow")
VMEM_LIMIT = 24 << 20


def attend(queries, k_cache, value_cache, lengths):
    reqs, heads, head_dim = queries.shape
    kv_heads = k_cache.shape[2]
    group = heads // kv_heads
    grouped = queries.reshape(reqs, kv_heads, group, head_dim)
    scores = jnp.einsum(
        "rkgd,rlkd->rkgl", grouped, k_cache, preferred_element_type=jnp.float32
    ) * head_dim ** (-0.5)
    valid = jnp.arange(k_cache.shape[1], dtype=jnp.int32)[None, :] < lengths[:, None]
    valid = valid[:, None, None, :]
    scores = jnp.where(valid, scores, -1e30)
    top = jnp.max(scores, axis=-1, keepdims=True)
    expd = jnp.where(valid, jnp.exp(scores - top), 0.0)
    probs = (expd / jnp.sum(expd, axis=-1, keepdims=True)).astype(jnp.bfloat16)
    mixed = jnp.einsum("rkgl,rlkd->rkgd", probs, value_cache, preferred_element_type=jnp.float32)
    return mixed.astype(jnp.bfloat16).reshape(reqs, heads * head_dim)


def pack_kernel(experts, spares, tokens, gate, ids, replica, out_ref, gate_ref, ids_ref, replica_ref, sem):
    rows, width = tokens.shape
    extra = out_ref.shape[1] - width
    copies = [
        pltpu.make_async_copy(gate, gate_ref, sem.at[0]),
        pltpu.make_async_copy(ids, ids_ref, sem.at[1]),
        pltpu.make_async_copy(replica, replica_ref, sem.at[2]),
        pltpu.make_async_copy(tokens, out_ref.at[:, pl.ds(0, width)], sem.at[3]),
    ]
    for copy in copies:
        copy.start()
    for copy in copies[:3]:
        copy.wait()
    slots = jnp.where(
        (replica_ref[...] == 1) & (ids_ref[...] < spares), ids_ref[...] + experts, ids_ref[...]
    )
    weights = gate_ref[...].astype(jnp.float32)
    slot = lax.broadcasted_iota(jnp.int32, (extra, rows), 0)
    coef = jnp.zeros((extra, rows), jnp.float32)
    for k in range(slots.shape[0]):
        coef = coef + jnp.where(slot == slots[k : k + 1, :], weights[k : k + 1, :], 0.0)
    out_ref[:, width:] = coef.T.astype(out_ref.dtype)
    copies[3].wait()


def pack(tokens, gate_wts, expert_ids, replica, devices):
    rows, width = tokens.shape
    top_count = gate_wts.shape[1]
    extra = pl.cdiv(SLOT_DEV * devices, LANES) * LANES
    return pl.pallas_call(
        functools.partial(pack_kernel, 3 * devices // 2, devices // 2),
        out_shape=jax.ShapeDtypeStruct((rows, width + extra), tokens.dtype),
        in_specs=[pl.BlockSpec(memory_space=pl.ANY)] * 4,
        out_specs=pl.BlockSpec(memory_space=pltpu.VMEM),
        scratch_shapes=[
            pltpu.VMEM((top_count, rows), gate_wts.dtype),
            pltpu.VMEM((top_count, rows), expert_ids.dtype),
            pltpu.VMEM((top_count, rows), replica.dtype),
            pltpu.SemaphoreType.DMA((4,)),
        ],
        compiler_params=pltpu.CompilerParams(vmem_limit_bytes=4 << 20),
        name="pack",
    )(*(pltpu.with_memory_space_constraint(v, pltpu.HBM) for v in (tokens, gate_wts.T, expert_ids.T, replica.T)))


def stage_kernel(first_ref, gate, up, down, gu_ref, down_ref, sem):
    slots, _, half = gate.shape
    copies = []
    for j in range(slots):
        copies.append(pltpu.make_async_copy(gate.at[j], gu_ref.at[j, :, pl.ds(0, half)], sem.at[j, 0]))
        copies.append(pltpu.make_async_copy(up.at[j], gu_ref.at[j, :, pl.ds(half, half)], sem.at[j, 1]))
        copies.append(pltpu.make_async_copy(down.at[j], down_ref.at[j], sem.at[j, 2]))
    for copy in copies:
        copy.start()
    for copy in copies:
        copy.wait()


def stage(first, gate, up, down):
    slots, width, half = gate.shape
    anywhere = pl.BlockSpec(memory_space=pl.ANY)
    return pl.pallas_call(
        stage_kernel,
        out_shape=[
            pltpu.VMEM((slots, width, 2 * half), gate.dtype),
            pltpu.VMEM((slots, half, width), down.dtype),
        ],
        in_specs=[pl.BlockSpec(memory_space=pltpu.SMEM)] + [anywhere] * 3,
        out_specs=[anywhere] * 2,
        scratch_shapes=[pltpu.SemaphoreType.DMA((slots, 3))],
        compiler_params=pltpu.CompilerParams(vmem_limit_bytes=4 << 20),
        name="stage",
    )(first, *(pltpu.with_memory_space_constraint(w, pltpu.HBM) for w in (gate, up, down)))


def expert_kernel(count, sources, base, with_sum, first_ref, *refs):
    blocks, refs = refs[:count], refs[count:]
    weights, refs = refs[: 2 * sources], refs[2 * sources :]
    sums, refs = (refs[:count], refs[count:]) if with_sum else ((), refs)
    outs, refs = refs[:count], refs[count:]
    x_ref, hidden_ref, x_sem = refs
    rows = blocks[0].shape[0]
    slots, half, width = weights[1].shape
    copies = [
        pltpu.make_async_copy(blocks[i], x_ref.at[pl.ds(i * rows, rows)], x_sem.at[i])
        for i in range(count)
    ]
    for copy in copies:
        copy.start()
    for copy in copies:
        copy.wait()
    shares = x_ref[:, width:].astype(jnp.float32)
    lane = lax.broadcasted_iota(jnp.int32, shares.shape, 1)
    result = None
    for n in range(sources):
        gu_ref, down_ref = weights[2 * n : 2 * n + 2]
        for j in range(slots):
            coef = jnp.sum(jnp.where(lane == first_ref[base + n] + j, shares, 0.0), axis=1, keepdims=True)
            both = jnp.dot(x_ref[:, :width], gu_ref[j], preferred_element_type=jnp.float32)
            gated, upward = both[:, :half], both[:, half:]
            hidden = gated / (1.0 + jnp.exp(-gated)) * upward * coef
            hidden_ref[:, j * half : (j + 1) * half] = hidden.astype(hidden_ref.dtype)
        down = down_ref[...].reshape(slots * half, width)
        part = jnp.dot(hidden_ref[...], down, preferred_element_type=jnp.float32)
        result = part if result is None else result + part
    for i in range(count):
        part = result[i * rows : (i + 1) * rows]
        if with_sum:
            part = part + sums[i][...]
        outs[i][...] = part.astype(outs[i].dtype)


def expert(blocks, weights, base, first, sums, dtype):
    count = len(blocks)
    sources = len(weights) // 2
    rows, packed = blocks[0].shape
    slots, half, width = weights[1].shape
    anywhere = pl.BlockSpec(memory_space=pl.ANY)
    whole = pl.BlockSpec(memory_space=pltpu.VMEM)
    weights = [pltpu.with_memory_space_constraint(w, pltpu.VMEM) for w in weights]
    return pl.pallas_call(
        functools.partial(expert_kernel, count, sources, base, bool(sums)),
        out_shape=[jax.ShapeDtypeStruct((rows, width), dtype)] * count,
        in_specs=[pl.BlockSpec(memory_space=pltpu.SMEM)]
        + [anywhere] * count
        + [whole] * (len(weights) + len(sums)),
        out_specs=[whole] * count,
        scratch_shapes=[
            pltpu.VMEM((count * rows, packed), blocks[0].dtype),
            pltpu.VMEM((count * rows, slots * half), blocks[0].dtype),
            pltpu.SemaphoreType.DMA((count,)),
        ],
        compiler_params=pltpu.CompilerParams(vmem_limit_bytes=VMEM_LIMIT),
        name="expert",
    )(first, *blocks, *weights, *sums)


def permutations(chips):
    ring = list(range(0, chips, 2)) + list(range(chips - 1 - chips % 2, 0, -2))
    ups = [2 * chip + place % 2 for place, chip in enumerate(ring)]
    downs = [2 * chip + (place + 1) % 2 for place, chip in enumerate(ring)]
    same, cross = [], []
    for place in range(chips):
        after = (place + 1) % chips
        same += [(ups[place], ups[after]), (downs[after], downs[place])]
        cross += [(downs[place], ups[after]), (ups[after], downs[place])]
    return same, cross, [(b, a) for a, b in same], [(b, a) for a, b in cross]


def local(
    tokens,
    gate_wts,
    expert_ids,
    replica,
    w_gate,
    w_up,
    w_down,
    queries,
    k_cache,
    value_cache,
    lengths,
):
    chips = lax.axis_size("wide")
    devices = chips * lax.axis_size("narrow")
    same, cross, same_back, cross_back = permutations(chips)
    far = chips // 2
    core = lax.axis_index("narrow")
    me = lax.axis_index("wide") * 2 + core
    mine_first = me * SLOT_DEV
    theirs_first = (me + 1 - 2 * core) * SLOT_DEV
    first = jnp.stack([mine_first, theirs_first]).astype(jnp.int32)
    own = pack(tokens, gate_wts, expert_ids, replica, devices)
    near_rows, far_rows = {}, {}
    near_rows[1] = lax.ppermute(own, AXES, same)
    far_rows[1] = lax.ppermute(own, AXES, cross)
    mine = list(stage(first, w_gate, w_up, w_down))
    theirs = []
    for w in mine:
        theirs.append(lax.ppermute(w, "narrow", [(0, 1), (1, 0)]))
    for k in range(2, far + 1):
        near_rows[k] = lax.ppermute(near_rows[k - 1], AXES, same)
        if k < far:
            far_rows[k] = lax.ppermute(far_rows[k - 1], AXES, same)
    rows_of = {("own", 0): own}
    rows_of.update({("near", k): v for k, v in near_rows.items()})
    rows_of.update({("far", k): v for k, v in far_rows.items()})
    partial = {}
    for group in groups_of(far):
        names = [n for k in group for n in names_of(k, far)]
        top = group[-1]
        if top == far:
            outs = expert([rows_of[n] for n in names], mine + theirs, 0, first, [], jnp.bfloat16)
            partial.update(zip(names, outs, strict=True))
            continue
        outs = expert([rows_of[n] for n in names], mine, 0, first, [], jnp.float32)
        outs = expert([rows_of[n] for n in names], theirs, 1, first, list(outs), jnp.bfloat16)
        partial.update(zip(names, outs, strict=True))
    near_sum = partial["near", far]
    far_sum = partial["far", far - 1]
    for k in range(far - 1, 0, -1):
        near_sum = lax.ppermute(near_sum, AXES, same_back)
        near_sum = add(near_sum, partial["near", k])
        if k < far - 1:
            far_sum = lax.ppermute(far_sum, AXES, same_back)
            far_sum = add(far_sum, partial["far", k])
    lengths, near_sum = lax.optimization_barrier((lengths, near_sum))
    near_sum = lax.ppermute(near_sum, AXES, same_back)
    far_sum = lax.ppermute(far_sum, AXES, cross_back)
    attn_out = attend(queries, k_cache, value_cache, lengths)
    routed_out = add(near_sum, far_sum, partial["own", 0])
    return (routed_out, attn_out)


def add(*values):
    return sum(v.astype(jnp.float32) for v in values).astype(jnp.bfloat16)


def groups_of(far):
    near = [list(range(k, min(k + 2, far - 2))) for k in range(0, far - 2, 2)]
    return [*near, [far - 2], [far - 1, far]]


def names_of(k, far):
    if k == 0:
        return [("own", 0)]
    return [("near", k), ("far", k)] if k < far else [("near", k)]


def solution(mesh):
    rows = P(("groups", "wide", "narrow"))
    slots = P(("wide", "narrow"))
    in_specs = (rows, rows, rows, rows, slots, slots, slots, rows, rows, rows, rows)
    return jax.shard_map(local, mesh=mesh, in_specs=in_specs, out_specs=(rows, rows), check_vma=False)
```

```python
import functools

import jax
import jax.numpy as jnp
from jax import lax
from jax.experimental import pallas as pl
from jax.experimental.pallas import tpu as pltpu
from jax.sharding import PartitionSpec as P


SLOT_DEV = 2
LANES = 128
TILE = 16
AXES = ("wide", "narrow")
VMEM_LIMIT = 24 << 20


def attend(queries, k_cache, value_cache, lengths):
    reqs, heads, head_dim = queries.shape
    kv_heads = k_cache.shape[2]
    group = heads // kv_heads
    grouped = queries.reshape(reqs, kv_heads, group, head_dim)
    scores = jnp.einsum(
        "rkgd,rlkd->rkgl", grouped, k_cache, preferred_element_type=jnp.float32
    ) * head_dim ** (-0.5)
    valid = jnp.arange(k_cache.shape[1], dtype=jnp.int32)[None, :] < lengths[:, None]
    valid = valid[:, None, None, :]
    scores = jnp.where(valid, scores, -1e30)
    top = jnp.max(scores, axis=-1, keepdims=True)
    expd = jnp.where(valid, jnp.exp(scores - top), 0.0)
    probs = (expd / jnp.sum(expd, axis=-1, keepdims=True)).astype(jnp.bfloat16)
    mixed = jnp.einsum("rkgl,rlkd->rkgd", probs, value_cache, preferred_element_type=jnp.float32)
    return mixed.astype(jnp.bfloat16).reshape(reqs, heads * head_dim)


def pack_kernel(experts, spares, tokens, gate, ids, replica, out_ref, rows_ref, gate_ref, ids_ref, replica_ref, sem):
    rows, width = tokens.shape
    copies = [
        pltpu.make_async_copy(gate, gate_ref, sem.at[0]),
        pltpu.make_async_copy(ids, ids_ref, sem.at[1]),
        pltpu.make_async_copy(replica, replica_ref, sem.at[2]),
        pltpu.make_async_copy(tokens, rows_ref, sem.at[3]),
    ]
    for copy in copies:
        copy.start()
    for copy in copies[:3]:
        copy.wait()
    across = width // LANES
    held = rows // TILE * across
    extra = out_ref.shape[0] - held
    turns = LANES // rows
    slots = jnp.where(
        (replica_ref[...] == 1) & (ids_ref[...] < spares), ids_ref[...] + experts, ids_ref[...]
    )
    slots = jnp.concatenate([slots] * turns, axis=1)
    weights = jnp.concatenate([gate_ref[...].astype(jnp.float32)] * turns, axis=1)
    shape = (extra * TILE, LANES)
    slot = turns * lax.broadcasted_iota(jnp.int32, shape, 0)
    slot = slot + lax.broadcasted_iota(jnp.int32, shape, 1) // rows
    coef = jnp.zeros(shape, jnp.float32)
    for k in range(slots.shape[0]):
        coef = coef + jnp.where(slot == slots[k : k + 1, :], weights[k : k + 1, :], 0.0)
    for c in range(extra):
        out_ref[held + c] = coef[c * TILE : (c + 1) * TILE].astype(out_ref.dtype)
    copies[3].wait()
    for i in range(rows // TILE):
        for j in range(across):
            out_ref[i * across + j] = rows_ref[
                i * TILE : (i + 1) * TILE, j * LANES : (j + 1) * LANES
            ]


def pack(tokens, gate_wts, expert_ids, replica, devices):
    rows, width = tokens.shape
    top_count = gate_wts.shape[1]
    tiles = rows // TILE * (width // LANES) + pl.cdiv(SLOT_DEV * devices * rows, TILE * LANES)
    return pl.pallas_call(
        functools.partial(pack_kernel, 3 * devices // 2, devices // 2),
        out_shape=jax.ShapeDtypeStruct((tiles, TILE, LANES), tokens.dtype),
        in_specs=[pl.BlockSpec(memory_space=pl.ANY)] * 4,
        out_specs=pl.BlockSpec(memory_space=pltpu.VMEM),
        scratch_shapes=[
            pltpu.VMEM((rows, width), tokens.dtype),
            pltpu.VMEM((top_count, rows), gate_wts.dtype),
            pltpu.VMEM((top_count, rows), expert_ids.dtype),
            pltpu.VMEM((top_count, rows), replica.dtype),
            pltpu.SemaphoreType.DMA((4,)),
        ],
        compiler_params=pltpu.CompilerParams(vmem_limit_bytes=4 << 20),
        name="pack",
    )(*(pltpu.with_memory_space_constraint(v, pltpu.HBM) for v in (tokens, gate_wts.T, expert_ids.T, replica.T)))


def stage_kernel(first_ref, gate, up, down, gu_ref, down_ref, sem):
    slots, _, half = gate.shape
    copies = []
    for j in range(slots):
        copies.append(pltpu.make_async_copy(gate.at[j], gu_ref.at[j, :, pl.ds(0, half)], sem.at[j, 0]))
        copies.append(pltpu.make_async_copy(up.at[j], gu_ref.at[j, :, pl.ds(half, half)], sem.at[j, 1]))
        copies.append(pltpu.make_async_copy(down.at[j], down_ref.at[j], sem.at[j, 2]))
    for copy in copies:
        copy.start()
    for copy in copies:
        copy.wait()


def stage(first, gate, up, down):
    slots, width, half = gate.shape
    anywhere = pl.BlockSpec(memory_space=pl.ANY)
    return pl.pallas_call(
        stage_kernel,
        out_shape=[
            pltpu.VMEM((slots, width, 2 * half), gate.dtype),
            pltpu.VMEM((slots, half, width), down.dtype),
        ],
        in_specs=[pl.BlockSpec(memory_space=pltpu.SMEM)] + [anywhere] * 3,
        out_specs=[anywhere] * 2,
        scratch_shapes=[pltpu.SemaphoreType.DMA((slots, 3))],
        compiler_params=pltpu.CompilerParams(vmem_limit_bytes=4 << 20),
        name="stage",
    )(first, *(pltpu.with_memory_space_constraint(w, pltpu.HBM) for w in (gate, up, down)))


def rows_in(block, rows, across):
    return jnp.concatenate(
        [
            jnp.concatenate([block[i * across + j] for j in range(across)], axis=1)
            for i in range(rows // TILE)
        ],
        axis=0,
    )


def shares_in(blocks, rows, held, slots):
    turns = LANES // rows
    lines = []
    for block in blocks:
        shares = jnp.concatenate([block[c] for c in range(held, block.shape[0])], axis=0)
        shares = shares.astype(jnp.float32)
        place = lax.broadcasted_iota(jnp.int32, shares.shape, 0)
        for slot in slots:
            mine = jnp.where(place == lax.div(slot, turns), shares, 0.0)
            lines.append(jnp.sum(mine, axis=0, keepdims=True))
    spare = -len(lines) % 8
    if spare:
        lines.append(jnp.zeros((spare, LANES), jnp.float32))
    columns = jnp.concatenate(lines, axis=0).T
    found = []
    for t, slot in enumerate(slots):
        turn = lax.rem(slot, turns)
        parts = []
        for i in range(len(blocks)):
            at = i * len(slots) + t
            column = columns[:, at : at + 1]
            pieces = [column[h * rows : (h + 1) * rows] for h in range(turns)]
            part = pieces[0]
            for h in range(1, turns):
                part = jnp.where(turn == h, pieces[h], part)
            parts.append(part)
        found.append(jnp.concatenate(parts, axis=0))
    return found


def expert_kernel(count, sources, base, with_sum, first_ref, *refs):
    blocks, refs = refs[:count], refs[count:]
    weights, refs = refs[: 2 * sources], refs[2 * sources :]
    sums, refs = (refs[:count], refs[count:]) if with_sum else ((), refs)
    outs, refs = refs[:count], refs[count:]
    hidden_ref, share_ref = refs
    rows = outs[0].shape[0]
    slots, half, width = weights[1].shape
    across = width // LANES
    held = rows // TILE * across
    numbers = [first_ref[base + n] + j for n in range(sources) for j in range(slots)]
    for t, column in enumerate(shares_in(blocks, rows, held, numbers)):
        share_ref[:, t : t + 1] = column
    x = jnp.concatenate([rows_in(block, rows, across) for block in blocks], axis=0)
    result = None
    for n in range(sources):
        gu_ref, down_ref = weights[2 * n : 2 * n + 2]
        for j in range(slots):
            t = n * slots + j
            coef = share_ref[:, t : t + 1]
            both = jnp.dot(x, gu_ref[j], preferred_element_type=jnp.float32)
            gated, upward = both[:, :half], both[:, half:]
            hidden = gated / (1.0 + jnp.exp(-gated)) * upward * coef
            hidden_ref[:, j * half : (j + 1) * half] = hidden.astype(hidden_ref.dtype)
        down = down_ref[...].reshape(slots * half, width)
        part = jnp.dot(hidden_ref[...], down, preferred_element_type=jnp.float32)
        result = part if result is None else result + part
    for i in range(count):
        part = result[i * rows : (i + 1) * rows]
        if with_sum:
            part = part + sums[i][...]
        outs[i][...] = part.astype(outs[i].dtype)


def expert(blocks, rows, weights, base, first, sums, dtype):
    count = len(blocks)
    sources = len(weights) // 2
    slots, half, width = weights[1].shape
    whole = pl.BlockSpec(memory_space=pltpu.VMEM)
    weights = [pltpu.with_memory_space_constraint(w, pltpu.VMEM) for w in weights]
    return pl.pallas_call(
        functools.partial(expert_kernel, count, sources, base, bool(sums)),
        out_shape=[jax.ShapeDtypeStruct((rows, width), dtype)] * count,
        in_specs=[pl.BlockSpec(memory_space=pltpu.SMEM)]
        + [whole] * (count + len(weights) + len(sums)),
        out_specs=[whole] * count,
        scratch_shapes=[
            pltpu.VMEM((count * rows, slots * half), blocks[0].dtype),
            pltpu.VMEM((count * rows, sources * slots), jnp.float32),
        ],
        compiler_params=pltpu.CompilerParams(vmem_limit_bytes=VMEM_LIMIT),
        name="expert",
    )(first, *blocks, *weights, *sums)


def permutations(chips):
    ring = list(range(0, chips, 2)) + list(range(chips - 1 - chips % 2, 0, -2))
    ups = [2 * chip + place % 2 for place, chip in enumerate(ring)]
    downs = [2 * chip + (place + 1) % 2 for place, chip in enumerate(ring)]
    same, cross = [], []
    for place in range(chips):
        after = (place + 1) % chips
        same += [(ups[place], ups[after]), (downs[after], downs[place])]
        cross += [(downs[place], ups[after]), (ups[after], downs[place])]
    return same, cross, [(b, a) for a, b in same], [(b, a) for a, b in cross]


def local(
    tokens,
    gate_wts,
    expert_ids,
    replica,
    w_gate,
    w_up,
    w_down,
    queries,
    k_cache,
    value_cache,
    lengths,
):
    chips = lax.axis_size("wide")
    devices = chips * lax.axis_size("narrow")
    same, cross, same_back, cross_back = permutations(chips)
    far = chips // 2
    core = lax.axis_index("narrow")
    me = lax.axis_index("wide") * 2 + core
    mine_first = me * SLOT_DEV
    theirs_first = (me + 1 - 2 * core) * SLOT_DEV
    first = jnp.stack([mine_first, theirs_first]).astype(jnp.int32)
    own = pack(tokens, gate_wts, expert_ids, replica, devices)
    near_rows, far_rows = {}, {}
    near_rows[1] = lax.ppermute(own, AXES, same)
    far_rows[1] = lax.ppermute(own, AXES, cross)
    mine = list(stage(first, w_gate, w_up, w_down))
    theirs = []
    for w in mine:
        theirs.append(lax.ppermute(w, "narrow", [(0, 1), (1, 0)]))
    for k in range(2, far + 1):
        near_rows[k] = lax.ppermute(near_rows[k - 1], AXES, same)
        if k < far:
            far_rows[k] = lax.ppermute(far_rows[k - 1], AXES, same)
    rows_of = {("own", 0): own}
    rows_of.update({("near", k): v for k, v in near_rows.items()})
    rows_of.update({("far", k): v for k, v in far_rows.items()})
    partial = {}
    for group in groups_of(far):
        names = [n for k in group for n in names_of(k, far)]
        top = group[-1]
        if top == far:
            names.remove(("near", far - 1))
        elif top == far - 2:
            names.append(("near", far - 1))
        if top == far:
            outs = expert([rows_of[n] for n in names], tokens.shape[0], mine + theirs, 0, first, [], jnp.bfloat16)
            partial.update(zip(names, outs, strict=True))
            continue
        outs = expert([rows_of[n] for n in names], tokens.shape[0], mine, 0, first, [], jnp.float32)
        outs = expert([rows_of[n] for n in names], tokens.shape[0], theirs, 1, first, list(outs), jnp.bfloat16)
        partial.update(zip(names, outs, strict=True))
    near_sum = partial["near", far]
    far_sum = partial["far", far - 1]
    for k in range(far - 1, 0, -1):
        near_sum = lax.ppermute(near_sum, AXES, same_back)
        near_sum = add(near_sum, partial["near", k])
        if k < far - 1:
            far_sum = lax.ppermute(far_sum, AXES, same_back)
            far_sum = add(far_sum, partial["far", k])
    lengths, near_sum = lax.optimization_barrier((lengths, near_sum))
    near_sum = lax.ppermute(near_sum, AXES, same_back)
    far_sum = lax.ppermute(far_sum, AXES, cross_back)
    attn_out = attend(queries, k_cache, value_cache, lengths)
    routed_out = add(near_sum, far_sum, partial["own", 0])
    return (routed_out, attn_out)


def add(*values):
    return sum(v.astype(jnp.float32) for v in values).astype(jnp.bfloat16)


def groups_of(far):
    near = [list(range(k, min(k + 2, far - 2))) for k in range(0, far - 2, 2)]
    return [*near, [far - 2], [far - 1, far]]


def names_of(k, far):
    if k == 0:
        return [("own", 0)]
    return [("near", k), ("far", k)] if k < far else [("near", k)]


def solution(mesh):
    rows = P(("groups", "wide", "narrow"))
    slots = P(("wide", "narrow"))
    in_specs = (rows, rows, rows, rows, slots, slots, slots, rows, rows, rows, rows)
    return jax.shard_map(local, mesh=mesh, in_specs=in_specs, out_specs=(rows, rows), check_vma=False)
```
